32 devices in a mesh: seq: 4 (over x, core), exp: 8 (over z, y).
Axes of the slice: x: 2, y: 2, z: 4, core: 2. Of those that a mesh axis runs over, the one named last changes fastest.
Arguments:
- mixer_input: bfloat16 [1024, 16384], P('seq', 'exp'), may hold values from -6 to 6
- mixer_gate: bfloat16 [1024, 16384], P('seq', 'exp'), may hold values from -6 to 6
- input_map: float32 [16, 1024], P(None, 'seq'), may hold values from -0.6 to 0.6
- output_map: float32 [16, 1024], P(None, 'seq'), may hold values from -1.5 to 1.5
- log_decay: float32 [256, 1024], P('exp', 'seq'), may hold values from -1 to 0, as said below
- skip_gain: float32 [256], P('exp'), may hold values from 0.5 to 1.5
- out_proj: bfloat16 [16384, 4096], P('exp', 'seq'), may hold values from -0.046875 to 0.046875
- residual: bfloat16 [1024, 4096], P(('seq', 'exp')), may hold values from -64 to 64
- norm_gain: float32 [4096], replicated, may hold values from 0.1 to 1.9
- router_weight: float32 [4, 4096], replicated, may hold values from -0.09375 to 0.09375
- expert_ids: int32 [1024, 2], P('seq'), may hold values from 0 to 3, all different within a row; in each aligned block of 32 rows (0 to 31, 32 to 63, ...) at most 32 rows name the same one
- gate_weight: bfloat16 [4, 4096, 12288], P('seq', None, 'exp'), may hold values from -0.09375 to 0.09375
- up_weight: bfloat16 [4, 4096, 12288], P('seq', None, 'exp'), may hold values from -0.09375 to 0.09375
- down_weight: bfloat16 [4, 12288, 4096], P('seq', 'exp'), may hold values from -0.0546875 to 0.0546875
Outputs:
- layer_out: bfloat16 [1024, 4096], P(('seq', 'exp'))
The draws below stay inside these ranges and needn't reach their ends.
Inputs may be any that keep to these rules, and one draw needn't show every extreme that they name: `expert_ids`: in every aligned block of 32 rows (the tokens one device holds in the output) each expert is named by at most 32 rows, a bound that some block reaches; the two ids of a row differ. `log_decay`: negative everywhere.
All inputs are finite; a program needn't handle non-finite values.
Results may differ from the reference program's by a relative error of at most 0.019.
Values may be sent and summed in bfloat16 or wider, within the bound.
No kernel may reach another device: no remote copies, remote signals or barrier semaphores. Data moves between devices by JAX's collectives and lax.ppermute only.
A program may use at most 128 MiB of HBM per device.

```python
import math
import jax
import jax.numpy as jnp
import numpy as np
from jax import lax

D = 4096
DI = 16384
HEAD = 64
STATE = 16
GROUP = 256
FF = 12288
SEQUENCE_LENGTH = 1024
TOK_DEV = 32
EXPERTS = 4
CAP = 32
FF_DEV = 1536
HEADS = 256
N_EXP = 8


def draw_log_decay(key, part):
    split_random_keys = jax.random.split(jax.random.fold_in(key, 11), 6)
    fast_share = 0.5
    is_fast = jax.random.uniform(split_random_keys[0], (HEADS,)) < fast_share
    slow_rate = jnp.exp(jax.random.uniform(split_random_keys[1], (HEADS,), minval=math.log(0.05 / SEQUENCE_LENGTH), maxval=math.log(0.5 / SEQUENCE_LENGTH)))
    fast_rate = jnp.exp(jax.random.uniform(split_random_keys[2], (HEADS,), minval=math.log(0.02), maxval=math.log(0.06)))
    decay_speed = jnp.where(is_fast, fast_rate, slow_rate)
    jitter_amplitude = jnp.exp(jax.random.uniform(split_random_keys[3], (HEADS, SEQUENCE_LENGTH), minval=math.log(0.5), maxval=math.log(2.0)))
    spike_locations = jax.random.randint(split_random_keys[4], (2,), 0, SEQUENCE_LENGTH)
    spike_height = jax.random.uniform(split_random_keys[5], (2,), minval=math.log(0.5), maxval=math.log(0.8))
    position_indices = jnp.arange(SEQUENCE_LENGTH)
    spike_component = jnp.sum(jnp.where(position_indices[None, :] == spike_locations[:, None], spike_height[:, None], 0.0), axis=0)
    return (-decay_speed[:, None] * jitter_amplitude + spike_component[None, :]).astype(jnp.float32)


def draw_residual(key, part):
    split_random_keys = jax.random.split(jax.random.fold_in(key, 23), 3)
    row_scale = jnp.exp(jax.random.uniform(split_random_keys[0], (SEQUENCE_LENGTH, 1), minval=math.log(0.3), maxval=math.log(3.0)))
    col_scale = jnp.exp(jax.random.uniform(split_random_keys[1], (1, D), minval=math.log(0.3), maxval=math.log(3.0)))
    values = jnp.clip(jax.random.normal(split_random_keys[2], (SEQUENCE_LENGTH, D)), -4.0, 4.0)
    return (values * row_scale * col_scale).astype(jnp.bfloat16)


def levels(rng, extent, cuts, smallest, top_value):
    def one(dim, shards_of):
        steps = jax.random.uniform(jax.random.fold_in(jax.random.fold_in(rng, 6), dim), (shards_of,), jnp.float32, smallest / len(cuts), top_value / len(cuts))
        return jnp.repeat(jnp.exp(steps), extent[dim] // shards_of).reshape((-1,) + (1,) * (len(extent) - dim - 1))

    factor_of = one(*cuts[0])
    for cut in cuts[1:]:
        factor_of = factor_of * one(*cut)
    return factor_of


def deal_out(own_key, own, number, rows, count, top, reach, lean):
    order = jax.random.permutation(own_key, count)
    packed, usual = shares(count, rows * top, reach, lean, True), shares(count, rows * top, reach, lean, False)
    places = jnp.arange(count)

    def named(sizes, turn):
        used = int((sizes > 0).sum())
        fixed = max(1, used // 4)
        shifted = fixed + (places - fixed + turn * (used - fixed)) % max(1, count - fixed)
        return jnp.zeros((count,), jnp.int32).at[order[jnp.where(places < fixed, places, shifted)]].set(jnp.asarray(sizes, jnp.int32))

    sizes = jnp.where(number % 4 == 0, named(packed, number // 4), named(usual, number - number // 4 - 1))
    mixed = jax.random.permutation(jax.random.fold_in(own, 3), count)
    source_of, taker = mixed[0:count // 2 * 2:2], mixed[1:count // 2 * 2:2]
    margin = jnp.minimum(sizes[source_of] - 1, reach - sizes[taker]) // 2
    margin = jnp.where((source_of == order[0]) | (taker == order[0]) | (sizes[taker] == 0), 0, jnp.maximum(margin, 0))
    shifted = jax.random.randint(jax.random.fold_in(own, 4), (count // 2,), 0, 1 << 20) % (margin + 1)
    sizes = sizes.at[source_of].add(-shifted).at[taker].add(shifted)
    items = jnp.searchsorted(jnp.cumsum(sizes), jnp.arange(rows * top), side="right").astype(jnp.int32)
    grid = items.reshape(top, rows).T
    grid = grid[jax.random.permutation(jax.random.fold_in(own, 1), rows)]
    turn = jax.random.randint(jax.random.fold_in(own, 2), (rows, 1), 0, top)
    return jnp.take_along_axis(grid, (jnp.arange(top)[None, :] + turn) % top, axis=1)


def shares(number_of, total, reach, skew, full):
    loads = [(1 << 20) // math.isqrt(standing ** skew) + 1 for standing in range(1, number_of + 1)]
    largest = reach if full else min(reach, max(-(-total // number_of), total * loads[0] // sum(loads)))
    least = 1 if total - largest >= number_of - 1 else 0
    given, spare = [largest] + [least] * (number_of - 1), total - largest - least * (number_of - 1)
    while spare > 0:
        candidates = [i for i in range(1, number_of) if given[i] < largest] or [i for i in range(1, number_of) if given[i] < reach]
        whole, remaining = sum([loads[i] for i in candidates]), spare
        for i in candidates:
            more = min(reach - given[i], max(1, remaining * loads[i] // whole), spare)
            given[i] = given[i] + more
            spare = spare - more
    return np.array(given)


def scatter_about(stream_key, shape, spread, most, cuts=(), kind=jnp.bfloat16):
    entries = jax.random.normal(stream_key, shape, jnp.float32) * spread
    if len(cuts) > 0:
        entries = levels(stream_key, shape, cuts, -0.22, 0.18) * entries
    return jnp.clip(entries, min=-most, max=most).astype(kind)


def setup_inputs(seed: int = 0) -> dict:
    seeds = jax.random.split(jax.random.key(seed), 15)
    mixer_input = scatter_about(seeds[0], (SEQUENCE_LENGTH, DI), 1.0, 6.0, ((0, 4), (1, 8)))
    mixer_gate = scatter_about(seeds[1], (SEQUENCE_LENGTH, DI), 1.0, 6.0, ((0, 4), (1, 8)))
    input_map = scatter_about(seeds[2], (STATE, SEQUENCE_LENGTH), 0.1, 0.6, ((1, 4),), jnp.float32)
    output_map = scatter_about(seeds[3], (STATE, SEQUENCE_LENGTH), 0.25, 1.5, ((1, 4),), jnp.float32)
    log_decay = draw_log_decay(jax.random.fold_in(seeds[14], 71), 0)
    skip_gain = jnp.clip(0.5 + 1.0 * jax.random.uniform(seeds[5], (HEADS,), jnp.float32) ** levels(seeds[5], (HEADS,), ((0, 8),), -0.2, 0.2), 0.5, 1.5)
    out_proj = scatter_about(seeds[6], (DI, D), DI ** -0.5, 0.046875, ((0, 8), (1, 4)))
    residual = draw_residual(jax.random.fold_in(seeds[14], 71), 0)
    norm_gain = jnp.clip(1.0 + 0.18 * jax.random.normal(seeds[8], (D,), jnp.float32), 0.1, 1.9)
    router_weight = scatter_about(seeds[9], (EXPERTS, D), D ** -0.5, 0.09375, (), jnp.float32)
    expert_ids_keys = jax.random.split(jax.random.fold_in(seeds[10], 1), SEQUENCE_LENGTH // TOK_DEV)
    expert_ids_turns = jax.random.permutation(jax.random.fold_in(seeds[10], 3), SEQUENCE_LENGTH // TOK_DEV)
    expert_ids = jax.vmap(lambda own, number: deal_out(jax.random.fold_in(seeds[10], 2), own, number, TOK_DEV, EXPERTS, 2, CAP, 2))(expert_ids_keys, expert_ids_turns).reshape((SEQUENCE_LENGTH, 2))
    gate_weight = scatter_about(seeds[11], (EXPERTS, D, FF), D ** -0.5, 0.09375, ((0, 4), (2, 8)))
    up_weight = scatter_about(seeds[12], (EXPERTS, D, FF), D ** -0.5, 0.09375, ((0, 4), (2, 8)))
    down_weight = scatter_about(seeds[13], (EXPERTS, FF, D), FF ** -0.5, 0.0546875, ((0, 4), (1, 8)))
    return {"mixer_input": mixer_input, "mixer_gate": mixer_gate, "input_map": input_map, "output_map": output_map, "log_decay": log_decay, "skip_gain": skip_gain, "out_proj": out_proj, "residual": residual, "norm_gain": norm_gain, "router_weight": router_weight, "expert_ids": expert_ids, "gate_weight": gate_weight, "up_weight": up_weight, "down_weight": down_weight}


epsilon = 1e-05

def group_parts(input_group, write_group, read_group, decay_group):
    group_len = decay_group.shape[1]
    cum_decay = jnp.cumsum(decay_group, axis=1)
    position_indices = jnp.arange(group_len, dtype=jnp.int32)
    causal = position_indices[:, None] >= position_indices[None, :]
    distance = cum_decay[:, :, None] - cum_decay[:, None, :]
    weights = jnp.where(causal[None], jnp.exp(jnp.where(causal[None], distance, 0.0)), 0.0)
    intersection = jnp.dot(read_group.T, write_group, precision=lax.Precision.HIGHEST)
    inner_part = jnp.einsum('hts,shp->thp', weights * intersection[None], input_group, precision=lax.Precision.HIGHEST)
    lead_decay = jnp.exp(cum_decay)
    tail_decay = jnp.exp(cum_decay[:, -1:] - cum_decay)
    local_state = jnp.einsum('hs,shp,ns->hpn', tail_decay, input_group, write_group, precision=lax.Precision.HIGHEST)
    return (inner_part, lead_decay, local_state, jnp.exp(cum_decay[:, -1]))

def apply_state(state_in, read_group, lead_decay):
    carried = jnp.einsum('hpn,nt->thp', state_in, read_group, precision=lax.Precision.HIGHEST)
    return carried * lead_decay.T[:, :, None]

def rms_scale(values, norm_gain):
    mean_sq = lax.optimization_barrier(jnp.mean(values * values, axis=1, keepdims=True))
    return (values * lax.rsqrt(mean_sq + epsilon) * norm_gain[None, :]).astype(jnp.bfloat16)

def pair_gates(normed, router_weight, first_id, second_id):
    logits = jnp.dot(normed.astype(jnp.float32), router_weight.T, precision=lax.Precision.HIGHEST)
    labels = jnp.arange(router_weight.shape[0], dtype=jnp.int32)
    left_logit = lax.optimization_barrier(jnp.sum(jnp.where(first_id[:, None] == labels[None, :], logits, 0.0), axis=1))
    right_logit = lax.optimization_barrier(jnp.sum(jnp.where(second_id[:, None] == labels[None, :], logits, 0.0), axis=1))
    return (jax.nn.sigmoid(left_logit - right_logit), jax.nn.sigmoid(right_logit - left_logit))

def reference(mixer_input, mixer_gate, input_map, output_map, log_decay, skip_gain, out_proj, residual, norm_gain, router_weight, expert_ids, gate_weight, up_weight, down_weight):
    seq_total = mixer_input.shape[0]
    blocks = seq_total // GROUP
    head_input = mixer_input.astype(jnp.float32).reshape(seq_total, HEADS, HEAD)
    input_blocks = head_input.reshape(blocks, GROUP, HEADS, HEAD)
    write_blocks = input_map.reshape(STATE, blocks, GROUP).transpose(1, 0, 2)
    read_blocks = output_map.reshape(STATE, blocks, GROUP).transpose(1, 0, 2)
    decay_blocks = log_decay.reshape(HEADS, blocks, GROUP).transpose(1, 0, 2)

    def advance(state_in, pieces):
        input_group, write_group, read_group, decay_group = pieces
        inner_part, lead_decay, local_state, group_decay = group_parts(input_group, write_group, read_group, decay_group)
        outputs = inner_part + apply_state(state_in, read_group, lead_decay)
        return (group_decay[:, None, None] * state_in + local_state, outputs)
    state_zero = jnp.zeros((HEADS, HEAD, STATE), jnp.float32)
    _, scanned = lax.scan(advance, state_zero, (input_blocks, write_blocks, read_blocks, decay_blocks))
    ssd_out = scanned.reshape(seq_total, HEADS, HEAD) + skip_gain[None, :, None] * head_input
    mamba_out = (ssd_out.reshape(seq_total, DI) * jax.nn.silu(mixer_gate.astype(jnp.float32))).astype(jnp.bfloat16)
    stream = jnp.dot(mamba_out, out_proj, preferred_element_type=jnp.float32) + residual.astype(jnp.float32)
    normed = rms_scale(stream, norm_gain)
    first_id = expert_ids[:, 0]
    second_id = expert_ids[:, 1]
    gate_first, gate_second = pair_gates(normed, router_weight, first_id, second_id)
    capacity = min(seq_total, seq_total // TOK_DEV * CAP)
    moe_out = jnp.zeros((seq_total, D), jnp.float32)
    for expert in range(EXPERTS):
        routed = (first_id == expert) | (second_id == expert)
        weight_row = jnp.where(first_id == expert, gate_first, 0.0) + jnp.where(second_id == expert, gate_second, 0.0)
        picked = jnp.nonzero(routed, size=capacity, fill_value=0)[0].astype(jnp.int32)
        is_valid = jnp.arange(capacity, dtype=jnp.int32) < jnp.sum(routed.astype(jnp.int32))
        chosen = normed[picked]
        gate_value = jnp.dot(chosen, gate_weight[expert], preferred_element_type=jnp.float32)
        up_value = jnp.dot(chosen, up_weight[expert], preferred_element_type=jnp.float32)
        activity = (jax.nn.silu(gate_value) * up_value).astype(jnp.bfloat16)
        act_slices = activity.reshape(capacity, N_EXP, FF_DEV).transpose(1, 0, 2)
        down_slices = down_weight[expert].reshape(N_EXP, FF_DEV, D)

        def add_slice(running, slice_pair):
            partial_value = jnp.dot(slice_pair[0], slice_pair[1], preferred_element_type=jnp.float32).astype(jnp.bfloat16)
            partial_value = lax.optimization_barrier(partial_value)
            return (running + partial_value.astype(jnp.float32), None)
        expert_out, _ = lax.scan(add_slice, jnp.zeros((capacity, D), jnp.float32), (act_slices, down_slices))
        scale_rows = jnp.where(is_valid, weight_row[picked], 0.0)
        moe_out = moe_out.at[picked].add(scale_rows[:, None] * expert_out)
    return (stream + moe_out).astype(jnp.bfloat16)
```

```python
import jax
import jax.numpy as jnp
from jax import lax
from jax.sharding import PartitionSpec as P

epsilon = 1e-05
BF = jnp.bfloat16
F32 = jnp.float32
LANES = 128
CHUNKS = 2


class Grid:
    def __init__(self, mesh):
        self.ns, self.ne = mesh.shape["seq"], mesh.shape["exp"]
        self.n = self.ns // 2
        self.nz = self.ne // self.n

    def split(self, i):
        s, e = divmod(i, self.ne)
        return s // 2, s % 2, e // self.n, e % self.n

    def join(self, x, c, z, y):
        return (x * 2 + c) * self.ne + z * self.n + y

    def swap(self, value, move):
        pairs = [(i, self.join(*move(*self.split(i)))) for i in range(self.ns * self.ne)]
        return lax.ppermute(value, ("seq", "exp"), pairs)

    def over_core(self, value):
        return self.swap(value, lambda x, c, z, y: (x, c ^ 1, z, y))

    def over_x(self, value, k):
        return self.swap(value, lambda x, c, z, y: (x ^ k, c, z, y))

    def over_y(self, value, k):
        return self.swap(value, lambda x, c, z, y: (x, c, z, y ^ k))

    def over_xy(self, value, k):
        return self.swap(
            value, lambda x, c, z, y: (x, c, z, y ^ k) if c else (x ^ k, c, z, y)
        )

    def over_yx(self, value, k):
        return self.swap(
            value, lambda x, c, z, y: (x ^ k, c, z, y) if c else (x, c, z, y ^ k)
        )

    def over_z(self, value):
        groups = [[z * self.n + y for z in range(self.nz)] for y in range(self.n)]
        return lax.all_to_all(value, "exp", 0, 0, axis_index_groups=groups)


def carried_state(grid, decay, state, seq):
    heads, width = state.shape
    own = jnp.concatenate(
        [state.astype(BF), jnp.broadcast_to(decay.astype(BF)[:, None], (heads, LANES))], axis=1
    )
    parts = [own] + [
        grid.swap(own, lambda x, c, z, y, k=k: ((x * 2 + c ^ k) // 2, (x * 2 + c ^ k) % 2, z, y))
        for k in range(1, grid.ns)
    ]
    stacked = jnp.stack(parts)
    before = jnp.zeros((heads, width), F32)
    for j in range(grid.ns - 1):
        part = lax.dynamic_index_in_dim(stacked, seq ^ j, 0, keepdims=False).astype(F32)
        new = part[:, width : width + 1] * before + part[:, :width]
        before = jnp.where(j < seq, new, before)
    return before


def mamba(grid, seq, mixer_input, mixer_gate, input_map, output_map, log_decay, skip_gain):
    rows, channels = mixer_input.shape
    heads = log_decay.shape[0]
    size = channels // heads
    states = input_map.shape[0]
    head_input = mixer_input.astype(F32).reshape(rows, heads, size)
    cum = jnp.cumsum(log_decay, axis=1)
    tail = jnp.exp(cum[:, -1:] - cum)
    local_state = jnp.einsum(
        "hs,shp,ns->hpn", tail, head_input, input_map, precision=lax.Precision.HIGHEST
    )
    incoming = carried_state(
        grid, jnp.exp(cum[:, -1]), local_state.reshape(heads, size * states), seq
    ).reshape(heads, size, states)
    positions = jnp.arange(rows, dtype=jnp.int32)
    causal = (positions[:, None] >= positions[None, :])[None]
    distance = cum[:, :, None] - cum[:, None, :]
    weights = jnp.where(causal, jnp.exp(jnp.where(causal, distance, 0.0)), 0.0)
    intersection = jnp.dot(output_map.T, input_map, precision=lax.Precision.HIGHEST)
    inner = jnp.einsum(
        "hts,shp->thp", weights * intersection[None], head_input, precision=lax.Precision.HIGHEST
    )
    carried = jnp.einsum("hpn,nt->thp", incoming, output_map, precision=lax.Precision.HIGHEST)
    carried = carried * jnp.exp(cum).T[:, :, None]
    ssd = inner + carried + skip_gain[None, :, None] * head_input
    return (ssd.reshape(rows, channels) * jax.nn.silu(mixer_gate.astype(F32))).astype(BF)


def gate_columns(normed, router_weight, ids):
    logits = jnp.dot(normed.astype(F32), router_weight.T, precision=lax.Precision.HIGHEST)
    labels = jnp.arange(router_weight.shape[0], dtype=jnp.int32)
    first = ids[:, :1] == labels[None, :]
    second = ids[:, 1:] == labels[None, :]
    left = jnp.sum(jnp.where(first, logits, 0.0), axis=1, keepdims=True)
    right = jnp.sum(jnp.where(second, logits, 0.0), axis=1, keepdims=True)
    return jnp.where(first, jax.nn.sigmoid(left - right), 0.0) + jnp.where(
        second, jax.nn.sigmoid(right - left), 0.0
    )


def shards(grid):
    n, nz = grid.n, grid.nz

    def run(
        mixer_input,
        mixer_gate,
        input_map,
        output_map,
        log_decay,
        skip_gain,
        out_proj,
        residual,
        norm_gain,
        router_weight,
        expert_ids,
        gate_weight,
        up_weight,
        down_weight,
    ):
        seq, exp = lax.axis_index("seq"), lax.axis_index("exp")
        x_at, core, y_at = seq // 2, seq % 2, exp % n
        tok, width = residual.shape
        cols = out_proj.shape[1]
        chunks = CHUNKS if tok % (16 * CHUNKS) == 0 else 1
        t = tok // chunks
        other_proj = grid.over_core(out_proj)
        mixed = mamba(
            grid, seq, mixer_input, mixer_gate, input_map, output_map, log_decay, skip_gain
        )
        mixed = mixed.reshape(nz, n, chunks, t, -1)
        own_ids = lax.dynamic_slice_in_dim(expert_ids, exp * tok, tok, 0)
        experts = grid.ns

        def first_half(h):
            mine = jnp.stack(
                [
                    lax.dynamic_index_in_dim(mixed[:, :, h], y_at ^ k, 1, keepdims=False)
                    for k in range(n)
                ]
            ).reshape(n * nz * t, -1)
            parts = [mine] + [grid.over_x(mine, k) for k in range(1, n)]
            sums = []
            for part in parts:
                both = [
                    jnp.dot(part, weight, preferred_element_type=F32)
                    for weight in (out_proj, other_proj)
                ]
                sums.append(jnp.concatenate(both, axis=1).reshape(n, nz, t, 2 * cols))
            total = jnp.stack([s[0] for s in sums])
            for k in range(1, n):
                sent = jnp.stack([s[k] for s in sums]).astype(BF)
                total = total + grid.over_y(sent, k).astype(F32)
            sent = total.astype(BF).transpose(1, 0, 2, 3)
            total = jnp.sum(grid.over_z(sent).astype(F32), axis=0)
            own_first = [total[0]] + [
                grid.over_x(total[k].astype(BF), k).astype(F32) for k in range(1, n)
            ]
            rows = jnp.stack(own_first).reshape(n, t, 2, cols)
            blocks = []
            for x in range(n):
                block = lax.dynamic_index_in_dim(rows, x_at ^ x, 0, keepdims=False)
                for c in range(2):
                    blocks.append(lax.dynamic_index_in_dim(block, core ^ c, 1, keepdims=False))
            here = slice(h * t, (h + 1) * t)
            stream = jnp.concatenate(blocks, axis=1) + residual[here].astype(F32)
            mean_sq = jnp.mean(stream * stream, axis=1, keepdims=True)
            normed = (stream * lax.rsqrt(mean_sq + epsilon) * norm_gain[None, :]).astype(BF)
            gates = gate_columns(normed, router_weight, own_ids[here])
            high = lax.reduce_precision(gates, 8, 7)
            low = gates - high
            spare = jnp.zeros((t, LANES - 2 * experts), BF)
            packed = jnp.concatenate([normed, high.astype(BF), low.astype(BF), spare], axis=1)
            return stream, packed

        def spread(packed):
            held = grid.over_z(jnp.broadcast_to(packed[None], (nz,) + packed.shape))
            held = jnp.stack([held] + [grid.over_xy(held, k) for k in range(1, n)])
            held = jnp.stack([held] + [grid.over_yx(held, k) for k in range(1, n)])
            return held, grid.over_core(held)

        def expert(held):
            flat = held.reshape(-1, held.shape[-1])
            tokens = flat[:, :width]
            tags = flat[:, width:].astype(F32)
            tags = tags[:, :experts] + tags[:, experts : 2 * experts]
            gate = lax.dynamic_slice_in_dim(tags, seq, 1, 1)
            hidden = jnp.dot(tokens, gate_weight[0], preferred_element_type=F32)
            hidden = jax.nn.silu(hidden) * jnp.dot(
                tokens, up_weight[0], preferred_element_type=F32
            )
            out = jnp.dot(hidden.astype(BF), down_weight[0], preferred_element_type=F32)
            return (out * gate).reshape(held.shape[:-1] + (width,))

        def gather_back(own, other):
            total = own + grid.over_core(other.astype(BF)).astype(F32)
            for move in (grid.over_yx, grid.over_xy):
                sent = total.astype(BF)
                total = total[0]
                for k in range(1, n):
                    total = total + move(sent[k], k).astype(F32)
            return jnp.sum(grid.over_z(total.astype(BF)).astype(F32), axis=0)

        outs = []
        for h in range(chunks):
            stream, packed = first_half(h)
            own, other = spread(packed)
            moe = gather_back(expert(own), expert(other))
            outs.append((stream + moe).astype(BF))
        return jnp.concatenate(outs, axis=0)

    return run


def solution(mesh):
    return jax.shard_map(
        shards(Grid(mesh)),
        mesh=mesh,
        in_specs=(
            P("seq", "exp"),
            P("seq", "exp"),
            P(None, "seq"),
            P(None, "seq"),
            P("exp", "seq"),
            P("exp"),
            P("exp", "seq"),
            P(("seq", "exp"), None),
            P(),
            P(),
            P("seq", None),
            P("seq", None, "exp"),
            P("seq", None, "exp"),
            P("seq", "exp", None),
        ),
        out_specs=P(("seq", "exp"), None),
        check_vma=False,
    )
```

```python
import math

import jax
import jax.numpy as jnp
from jax import lax
from jax.experimental import pallas as pl
from jax.experimental.pallas import tpu as pltpu
from jax.sharding import PartitionSpec as P


epsilon = 1e-05
BF = jnp.bfloat16
F32 = jnp.float32
LANES = 128
WIDE = 512
CHUNKS = 2


class Grid:
    def __init__(self, mesh):
        self.ns, self.ne = mesh.shape["seq"], mesh.shape["exp"]
        self.n = self.ns // 2
        self.nz = self.ne // self.n

    def split(self, i):
        s, e = divmod(i, self.ne)
        return s // 2, s % 2, e // self.n, e % self.n

    def join(self, x, c, z, y):
        return (x * 2 + c) * self.ne + z * self.n + y

    def swap(self, value, move):
        pairs = [(i, self.join(*move(*self.split(i)))) for i in range(self.ns * self.ne)]
        return lax.ppermute(value, ("seq", "exp"), pairs)

    def over_core(self, value):
        return self.swap(value, lambda x, c, z, y: (x, c ^ 1, z, y))

    def over_x(self, value, k):
        return self.swap(value, lambda x, c, z, y: (x ^ k, c, z, y))

    def over_y(self, value, k):
        return self.swap(value, lambda x, c, z, y: (x, c, z, y ^ k))

    def over_xy(self, value, k):
        return self.swap(
            value, lambda x, c, z, y: (x, c, z, y ^ k) if c else (x ^ k, c, z, y)
        )

    def over_yx(self, value, k):
        return self.swap(
            value, lambda x, c, z, y: (x ^ k, c, z, y) if c else (x, c, z, y ^ k)
        )

    def over_z(self, value, k):
        return self.swap(value, lambda x, c, z, y: (x, c, z ^ k, y))


def lane_halves(values, width):
    lane = lax.broadcasted_iota(jnp.int32, (1, width), 1)
    size = width // len(values)
    out = values[0]
    for j in range(1, len(values)):
        out = jnp.where(lane >= j * size, values[j], out)
    return out


def column(table, h):
    lane = lax.broadcasted_iota(jnp.int32, table.shape, 1)
    return jnp.sum(jnp.where(lane == h, table, 0.0), axis=1, keepdims=True)


def local_states(mixer_input, input_map, log_decay):
    rows, channels = mixer_input.shape
    heads, states = log_decay.shape[0], input_map.shape[0]
    per = LANES * heads // channels

    def kernel(x_ref, write_ref, decay_ref, cum_ref, turned_ref, sent_ref):
        at = lax.broadcasted_iota(jnp.int32, (rows, rows), 0)
        to = lax.broadcasted_iota(jnp.int32, (rows, rows), 1)
        decay = decay_ref[...]
        cum = jnp.dot(
            decay,
            jnp.where(at <= to, 1.0, 0.0),
            precision=lax.Precision.HIGHEST,
            preferred_element_type=F32,
        )
        cum_ref[...] = cum
        turned_ref[...] = lax.dot_general(
            jnp.where(to <= at, 1.0, 0.0),
            decay,
            (((1,), (1,)), ((), ())),
            precision=lax.Precision.HIGHEST,
            preferred_element_type=F32,
        )
        last = cum[:, rows - 1 :]
        tail = jnp.exp(last - cum)
        whole = jnp.exp(last)
        write = write_ref[...]
        for i in range(heads // per):
            lanes = slice(i * LANES, (i + 1) * LANES)
            here = range(i * per, (i + 1) * per)
            scaled = jnp.concatenate([tail[h : h + 1] * write for h in here], axis=0)
            out = jnp.dot(scaled.astype(BF), x_ref[:, lanes], preferred_element_type=F32)
            parts = [out[j * states : (j + 1) * states] for j in range(per)]
            sent_ref[:states, lanes] = lane_halves(parts, LANES).astype(BF)
            decays = lane_halves([whole[h : h + 1] for h in here], LANES)
            sent_ref[states:, lanes] = jnp.broadcast_to(decays, (8, LANES)).astype(BF)

    return pl.pallas_call(
        kernel,
        out_shape=(
            jax.ShapeDtypeStruct((heads, rows), F32),
            jax.ShapeDtypeStruct((rows, heads), F32),
            jax.ShapeDtypeStruct((states + 8, channels), BF),
        ),
        name="local_states",
    )(mixer_input, input_map, log_decay)


def inner_part(mixer_input, input_map, output_map, cum, turned, skip_gain):
    rows, channels = mixer_input.shape
    heads = cum.shape[0]
    per = LANES * heads // channels
    wide = math.gcd(channels, WIDE)

    def kernel(skip_ref, x_ref, write_ref, read_ref, cum_ref, turned_ref, out_ref, both_ref):
        i = pl.program_id(0)

        @pl.when(i == 0)
        def _():
            at = lax.broadcasted_iota(jnp.int32, (rows, rows), 0)
            to = lax.broadcasted_iota(jnp.int32, (rows, rows), 1)
            both = lax.dot_general(
                read_ref[...],
                write_ref[...],
                (((0,), (0,)), ((), ())),
                precision=lax.Precision.HIGHEST,
                preferred_element_type=F32,
            )
            both_ref[...] = jnp.where(at >= to, both, 0.0)

        turned = turned_ref[...]
        for p in range(wide // LANES):
            lanes = slice(p * LANES, (p + 1) * LANES)
            x = x_ref[:, lanes]
            outs, skips = [], []
            for j in range(per):
                h = (i * (wide // LANES) + p) * per + j
                distance = column(turned, h) - cum_ref[pl.ds(h, 1), :]
                weights = (jnp.exp(jnp.minimum(distance, 0.0)) * both_ref[...]).astype(BF)
                outs.append(jnp.dot(weights, x, preferred_element_type=F32))
                skips.append(jnp.full((1, LANES), skip_ref[h], F32))
            out_ref[:, lanes] = lane_halves(outs, LANES) + lane_halves(skips, LANES) * x.astype(F32)

    whole = lambda a: pl.BlockSpec(a.shape, lambda i, s: (0, 0))
    block = pl.BlockSpec((rows, wide), lambda i, s: (0, i))
    return pl.pallas_call(
        kernel,
        out_shape=jax.ShapeDtypeStruct((rows, channels), F32),
        grid_spec=pltpu.PrefetchScalarGridSpec(
            num_scalar_prefetch=1,
            grid=(channels // wide,),
            in_specs=[block, whole(input_map), whole(output_map), whole(cum), whole(turned)],
            out_specs=block,
            scratch_shapes=[pltpu.VMEM((rows, rows), F32)],
        ),
        name="inner_part",
    )(skip_gain, mixer_input, input_map, output_map, cum, turned)


def with_carried(seq, inner, mixer_gate, output_map, turned, parts):
    rows, channels = inner.shape
    heads, states = turned.shape[1], output_map.shape[0]
    per = LANES * heads // channels
    wide = math.gcd(channels, WIDE)
    shards_before = len(parts) - 1

    def kernel(seq_ref, inner_ref, gate_ref, read_ref, turned_ref, *refs):
        i, own = pl.program_id(0), seq_ref[0]
        part_refs, out_ref = refs[:-1], refs[-1]
        values = [ref[...].astype(F32) for ref in part_refs]
        before = jnp.zeros((states, wide), F32)
        for j in range(shards_before):
            part = values[0]
            for k in range(1, len(values)):
                part = jnp.where((own ^ j) == k, values[k], part)
            new = part[states : states + 1] * before + part[:states]
            before = jnp.where(j < own, new, before)
        carried = lax.dot_general(
            read_ref[...],
            before,
            (((0,), (0,)), ((), ())),
            precision=lax.Precision.HIGHEST,
            preferred_element_type=F32,
        )
        lead = jnp.exp(turned_ref[...])
        for p in range(wide // LANES):
            lanes = slice(p * LANES, (p + 1) * LANES)
            first = (i * (wide // LANES) + p) * per
            leads = lane_halves([column(lead, first + j) for j in range(per)], LANES)
            ssd = inner_ref[:, lanes] + carried[:, lanes] * leads
            out_ref[:, lanes] = (ssd * jax.nn.silu(gate_ref[:, lanes].astype(F32))).astype(BF)

    whole = lambda a: pl.BlockSpec(a.shape, lambda i, s: (0, 0))
    block = pl.BlockSpec((rows, wide), lambda i, s: (0, i))
    thin = pl.BlockSpec((states + 8, wide), lambda i, s: (0, i))
    return pl.pallas_call(
        kernel,
        out_shape=jax.ShapeDtypeStruct((rows, channels), BF),
        grid_spec=pltpu.PrefetchScalarGridSpec(
            num_scalar_prefetch=1,
            grid=(channels // wide,),
            in_specs=[block, block, whole(output_map), whole(turned)] + [thin] * len(parts),
            out_specs=block,
        ),
        name="with_carried",
    )(seq.reshape(1), inner, mixer_gate, output_map, turned, *parts)


def mamba(grid, seq, mixer_input, mixer_gate, input_map, output_map, log_decay, skip_gain):
    cum, turned, own = local_states(mixer_input, input_map, log_decay)
    parts = [own]
    for k in range(1, grid.ns):
        parts.append(
            grid.swap(
                own,
                lambda x, c, z, y, k=k: ((x * 2 + c ^ k) // 2, (x * 2 + c ^ k) % 2, z, y),
            )
        )
    inner = inner_part(mixer_input, input_map, output_map, cum, turned, skip_gain)
    return with_carried(seq, inner, mixer_gate, output_map, turned, parts)


def activity(seq, pieces, gate_weight, up_weight, experts, calls):
    part, packed = pieces[0].shape
    _, width, hidden = gate_weight.shape
    rows = part * len(pieces)
    wide = math.gcd(hidden, 256)
    steps = hidden // wide
    first = -(-steps // calls)

    def kernel(seq_ref, *refs):
        refs, (out_ref, tag_ref, x_ref, sems) = refs[:-4], refs[-4:]
        part_refs, (gate_ref, up_ref) = refs[: len(pieces)], refs[len(pieces) : len(pieces) + 2]

        @pl.when(pl.program_id(0) == 0)
        def _():
            copies = [
                pltpu.make_async_copy(ref, x_ref.at[pl.ds(i * part, part)], sems.at[i])
                for i, ref in enumerate(part_refs)
            ]
            for copy in copies:
                copy.start()
            for copy in copies:
                copy.wait()
            tags = x_ref[:, width:].astype(F32)
            lane = lax.broadcasted_iota(jnp.int32, tags.shape, 1)
            mine = (lane == seq_ref[0]) | (lane == seq_ref[0] + experts)
            tag = jnp.sum(jnp.where(mine, tags, 0.0), axis=1, keepdims=True)
            tag_ref[...] = jnp.broadcast_to(tag, tag_ref.shape)

        x = x_ref[:, :width]
        gate = jnp.dot(x, gate_ref[...], preferred_element_type=F32)
        up = jnp.dot(x, up_ref[...], preferred_element_type=F32)
        out_ref[...] = (jax.nn.silu(gate) * up).astype(BF)

    def call(start, count, done):
        weight = pl.BlockSpec((None, width, wide), lambda i, s: (0, 0, i + start))
        anywhere = pl.BlockSpec(memory_space=pl.ANY)
        inputs = list(pieces) + [gate_weight, up_weight] + done
        return pl.pallas_call(
            kernel,
            out_shape=(
                jax.ShapeDtypeStruct((rows, hidden), BF),
                jax.ShapeDtypeStruct((rows, LANES), F32),
            ),
            grid_spec=pltpu.PrefetchScalarGridSpec(
                num_scalar_prefetch=1,
                grid=(count,),
                in_specs=[anywhere] * len(pieces) + [weight, weight] + [anywhere] * len(done),
                out_specs=(
                    pl.BlockSpec((rows, wide), lambda i, s: (0, i + start)),
                    pl.BlockSpec((rows, LANES), lambda i, s: (0, 0)),
                ),
                scratch_shapes=[
                    pltpu.VMEM((rows, packed), BF),
                    pltpu.SemaphoreType.DMA((len(pieces),)),
                ],
            ),
            input_output_aliases={len(inputs): 0} if done else {},
            name="activity",
        )(seq.reshape(1), *inputs)

    out, tag = call(0, first, [])
    if steps > first:
        out, _ = call(first, steps - first, [out])
    return out, tag[:, :1]


def gate_columns(normed, router_weight, ids):
    logits = jnp.dot(normed.astype(F32), router_weight.T, precision=lax.Precision.HIGHEST)
    labels = jnp.arange(router_weight.shape[0], dtype=jnp.int32)
    first = ids[:, :1] == labels[None, :]
    second = ids[:, 1:] == labels[None, :]
    left = jnp.sum(jnp.where(first, logits, 0.0), axis=1, keepdims=True)
    right = jnp.sum(jnp.where(second, logits, 0.0), axis=1, keepdims=True)
    return jnp.where(first, jax.nn.sigmoid(left - right), 0.0) + jnp.where(
        second, jax.nn.sigmoid(right - left), 0.0
    )


def shards(grid):
    n, nz = grid.n, grid.nz

    def run(
        mixer_input,
        mixer_gate,
        input_map,
        output_map,
        log_decay,
        skip_gain,
        out_proj,
        residual,
        norm_gain,
        router_weight,
        expert_ids,
        gate_weight,
        up_weight,
        down_weight,
    ):
        seq, exp = lax.axis_index("seq"), lax.axis_index("exp")
        x_at, core, y_at, z_at = seq // 2, seq % 2, exp % n, exp // n
        tok, width = residual.shape
        cols = out_proj.shape[1]
        chunks = CHUNKS if tok % (16 * CHUNKS) == 0 else 1
        t = tok // chunks
        other_proj = grid.over_core(out_proj)
        mixed = mamba(
            grid, seq, mixer_input, mixer_gate, input_map, output_map, log_decay, skip_gain
        )
        mixed = mixed.reshape(nz, n, chunks, t, -1)
        own_ids = lax.dynamic_slice_in_dim(expert_ids, exp * tok, tok, 0)
        experts = grid.ns

        def first_half(h, before):
            mine = jnp.stack(
                [
                    lax.dynamic_index_in_dim(mixed[:, :, h], y_at ^ k, 1, keepdims=False)
                    for k in range(n)
                ]
            ).reshape(n * nz * t, -1)
            parts = [mine] + [grid.over_x(mine, k) for k in range(1, n)]
            sums = []
            for part in parts:
                both = [
                    jnp.dot(part, weight, preferred_element_type=F32)
                    for weight in (out_proj, other_proj)
                ]
                sums.append(jnp.concatenate(both, axis=1).reshape(n, nz, t, 2 * cols))
            total = jnp.stack([s[0] for s in sums])
            for k in range(1, n):
                sent = jnp.stack([s[k] for s in sums]).astype(BF)
                got = grid.over_y(sent, k)
                total = total + got.astype(F32)
            at_z = [
                lax.dynamic_index_in_dim(total, z_at ^ k, 1, keepdims=False) for k in range(nz)
            ]
            got = [grid.over_z(at_z[k].astype(BF), k) for k in range(1, nz)]
            got, _ = lax.optimization_barrier((got, before))
            total = at_z[0] + sum(g.astype(F32) for g in got)
            own_first = [total[0]] + [
                grid.over_x(total[k].astype(BF), k).astype(F32) for k in range(1, n)
            ]
            rows = jnp.stack(own_first).reshape(n, t, 2, cols)
            blocks = []
            for x in range(n):
                block = lax.dynamic_index_in_dim(rows, x_at ^ x, 0, keepdims=False)
                for c in range(2):
                    blocks.append(lax.dynamic_index_in_dim(block, core ^ c, 1, keepdims=False))
            here = slice(h * t, (h + 1) * t)
            stream = jnp.concatenate(blocks, axis=1) + residual[here].astype(F32)
            mean_sq = jnp.mean(stream * stream, axis=1, keepdims=True)
            normed = (stream * lax.rsqrt(mean_sq + epsilon) * norm_gain[None, :]).astype(BF)
            gates = gate_columns(normed, router_weight, own_ids[here])
            high = lax.reduce_precision(gates, 8, 7)
            low = gates - high
            spare = jnp.zeros((t, LANES - 2 * experts), BF)
            packed = jnp.concatenate([normed, high.astype(BF), low.astype(BF), spare], axis=1)
            return stream, packed

        def spread(packed):
            held = [packed] + [grid.over_z(packed, k) for k in range(1, nz)]
            held = lax.optimization_barrier(jnp.concatenate(held, axis=0))
            got = [grid.over_xy(held, k) for k in range(1, n)]
            held = jnp.concatenate([held] + got, axis=0)
            mine = [held] + [grid.over_yx(held, k) for k in range(1, n)]
            pieces = []
            for piece in mine:
                pieces += [piece, grid.over_core(piece)]
            return pieces

        def expert(pieces, calls):
            hidden, gate = activity(seq, pieces, gate_weight, up_weight, experts, calls)
            rows = hidden.shape[0] // n
            outs = []
            for k in reversed(range(n)):
                here = slice(k * rows, (k + 1) * rows)
                out = jnp.dot(hidden[here], down_weight[0], preferred_element_type=F32)
                out = lax.optimization_barrier(out)
                out = (out * gate[here]).astype(BF)
                outs.insert(0, (out[: rows // 2], out[rows // 2 :]))
            return outs

        def gather_back(outs):
            total = None
            for k, out in reversed(list(enumerate(outs))):
                got = grid.over_core(out[1])
                piece = out[0].astype(F32) + got.astype(F32)
                if k:
                    piece = grid.over_yx(piece.astype(BF), k).astype(F32)
                total = piece if total is None else total + piece
            total = total.reshape(n, -1, width)
            sent = total.astype(BF)
            total = total[0]
            for k in range(1, n):
                got = grid.over_xy(sent[k], k)
                total = total + got.astype(F32)
            total = total.reshape(nz, -1, width)
            got = [grid.over_z(total[k].astype(BF), k) for k in range(1, nz)]
            return total[0] + sum(g.astype(F32) for g in got)

        outs = []
        packed = residual
        for h in range(chunks):
            stream, packed = first_half(h, packed)
            done = expert(spread(packed), chunks - h)
            outs.append((stream, gather_back(done)))
        outs = lax.optimization_barrier(outs)
        return jnp.concatenate([(stream + moe).astype(BF) for stream, moe in outs], axis=0)

    return run


def solution(mesh):
    return jax.shard_map(
        shards(Grid(mesh)),
        mesh=mesh,
        in_specs=(
            P("seq", "exp"),
            P("seq", "exp"),
            P(None, "seq"),
            P(None, "seq"),
            P("exp", "seq"),
            P("exp"),
            P("exp", "seq"),
            P(("seq", "exp"), None),
            P(),
            P(),
            P("seq", None),
            P("seq", None, "exp"),
            P("seq", None, "exp"),
            P("seq", "exp", None),
        ),
        out_specs=P(("seq", "exp"), None),
        check_vma=False,
    )
```

```python
import math

import jax
import jax.numpy as jnp
from jax import lax
from jax.experimental import pallas as pl
from jax.experimental.pallas import tpu as pltpu
from jax.sharding import PartitionSpec as P


epsilon = 1e-05
BF = jnp.bfloat16
F32 = jnp.float32
LANES = 128
WIDE = 1024
CHUNKS = 2


class Grid:
    def __init__(self, mesh):
        self.ns, self.ne = mesh.shape["seq"], mesh.shape["exp"]
        self.n = self.ns // 2
        self.nz = self.ne // self.n

    def split(self, i):
        s, e = divmod(i, self.ne)
        return s // 2, s % 2, e // self.n, e % self.n

    def join(self, x, c, z, y):
        return (x * 2 + c) * self.ne + z * self.n + y

    def swap(self, value, move):
        pairs = [(i, self.join(*move(*self.split(i)))) for i in range(self.ns * self.ne)]
        return lax.ppermute(value, ("seq", "exp"), pairs)

    def over_core(self, value):
        return self.swap(value, lambda x, c, z, y: (x, c ^ 1, z, y))

    def over_x(self, value, k):
        return self.swap(value, lambda x, c, z, y: (x ^ k, c, z, y))

    def over_y(self, value, k):
        return self.swap(value, lambda x, c, z, y: (x, c, z, y ^ k))

    def over_xy(self, value, k):
        return self.swap(
            value, lambda x, c, z, y: (x, c, z, y ^ k) if c else (x ^ k, c, z, y)
        )

    def over_yx(self, value, k):
        return self.swap(
            value, lambda x, c, z, y: (x ^ k, c, z, y) if c else (x, c, z, y ^ k)
        )

    def over_z(self, value, k):
        return self.swap(value, lambda x, c, z, y: (x, c, z ^ k, y))


def lane_halves(values, width):
    lane = lax.broadcasted_iota(jnp.int32, (1, width), 1)
    size = width // len(values)
    out = values[0]
    for j in range(1, len(values)):
        out = jnp.where(lane >= j * size, values[j], out)
    return out


def column(table, h):
    lane = lax.broadcasted_iota(jnp.int32, table.shape, 1)
    return jnp.sum(jnp.where(lane == h, table, 0.0), axis=1, keepdims=True)


def local_states(mixer_input, input_map, log_decay):
    rows, channels = mixer_input.shape
    heads, states = log_decay.shape[0], input_map.shape[0]
    per = LANES * heads // channels

    def kernel(x_ref, write_ref, decay_ref, cum_ref, turned_ref, sent_ref):
        at = lax.broadcasted_iota(jnp.int32, (rows, rows), 0)
        to = lax.broadcasted_iota(jnp.int32, (rows, rows), 1)
        decay = decay_ref[...]
        cum = jnp.dot(
            decay,
            jnp.where(at <= to, 1.0, 0.0),
            precision=lax.Precision.HIGHEST,
            preferred_element_type=F32,
        )
        cum_ref[...] = cum
        turned_ref[...] = lax.dot_general(
            jnp.where(to <= at, 1.0, 0.0),
            decay,
            (((1,), (1,)), ((), ())),
            precision=lax.Precision.HIGHEST,
            preferred_element_type=F32,
        )
        last = cum[:, rows - 1 :]
        tail = jnp.exp(last - cum)
        whole = jnp.exp(last)
        write = write_ref[...]
        for i in range(heads // per):
            lanes = slice(i * LANES, (i + 1) * LANES)
            here = range(i * per, (i + 1) * per)
            scaled = jnp.concatenate([tail[h : h + 1] * write for h in here], axis=0)
            out = jnp.dot(scaled.astype(BF), x_ref[:, lanes], preferred_element_type=F32)
            parts = [out[j * states : (j + 1) * states] for j in range(per)]
            sent_ref[:states, lanes] = lane_halves(parts, LANES).astype(BF)
            decays = lane_halves([whole[h : h + 1] for h in here], LANES)
            sent_ref[states:, lanes] = jnp.broadcast_to(decays, (8, LANES)).astype(BF)

    return pl.pallas_call(
        kernel,
        out_shape=(
            jax.ShapeDtypeStruct((heads, rows), F32),
            jax.ShapeDtypeStruct((rows, heads), F32),
            jax.ShapeDtypeStruct((states + 8, channels), BF),
        ),
        name="local_states",
    )(mixer_input, input_map, log_decay)


def inner_part(mixer_input, input_map, output_map, cum, turned, skip_gain):
    rows, channels = mixer_input.shape
    heads = cum.shape[0]
    per = LANES * heads // channels
    wide = math.gcd(channels, WIDE)

    def kernel(skip_ref, x_ref, write_ref, read_ref, cum_ref, turned_ref, out_ref, both_ref):
        i = pl.program_id(0)

        @pl.when(i == 0)
        def _():
            at = lax.broadcasted_iota(jnp.int32, (rows, rows), 0)
            to = lax.broadcasted_iota(jnp.int32, (rows, rows), 1)
            both = lax.dot_general(
                read_ref[...],
                write_ref[...],
                (((0,), (0,)), ((), ())),
                precision=lax.Precision.HIGHEST,
                preferred_element_type=F32,
            )
            both_ref[...] = jnp.where(at >= to, both, 0.0)

        turned = turned_ref[...]
        for p in range(wide // LANES):
            lanes = slice(p * LANES, (p + 1) * LANES)
            x = x_ref[:, lanes]
            outs, skips = [], []
            for j in range(per):
                h = (i * (wide // LANES) + p) * per + j
                distance = column(turned, h) - cum_ref[pl.ds(h, 1), :]
                weights = (jnp.exp(jnp.minimum(distance, 0.0)) * both_ref[...]).astype(BF)
                outs.append(jnp.dot(weights, x, preferred_element_type=F32))
                skips.append(jnp.full((1, LANES), skip_ref[h], F32))
            out_ref[:, lanes] = lane_halves(outs, LANES) + lane_halves(skips, LANES) * x.astype(F32)

    whole = lambda a: pl.BlockSpec(a.shape, lambda i, s: (0, 0))
    block = pl.BlockSpec((rows, wide), lambda i, s: (0, i))
    return pl.pallas_call(
        kernel,
        out_shape=jax.ShapeDtypeStruct((rows, channels), F32),
        grid_spec=pltpu.PrefetchScalarGridSpec(
            num_scalar_prefetch=1,
            grid=(channels // wide,),
            in_specs=[block, whole(input_map), whole(output_map), whole(cum), whole(turned)],
            out_specs=block,
            scratch_shapes=[pltpu.VMEM((rows, rows), F32)],
        ),
        name="inner_part",
    )(skip_gain, mixer_input, input_map, output_map, cum, turned)


def with_carried(seq, inner, mixer_gate, output_map, turned, parts):
    rows, channels = inner.shape
    heads, states = turned.shape[1], output_map.shape[0]
    per = LANES * heads // channels
    wide = math.gcd(channels, WIDE)
    shards_before = len(parts) - 1

    def kernel(seq_ref, inner_ref, gate_ref, read_ref, turned_ref, *refs):
        i, own = pl.program_id(0), seq_ref[0]
        part_refs, out_ref = refs[:-1], refs[-1]
        values = [ref[...].astype(F32) for ref in part_refs]
        before = jnp.zeros((states, wide), F32)
        for j in range(shards_before):
            part = values[0]
            for k in range(1, len(values)):
                part = jnp.where((own ^ j) == k, values[k], part)
            new = part[states : states + 1] * before + part[:states]
            before = jnp.where(j < own, new, before)
        carried = lax.dot_general(
            read_ref[...].astype(BF),
            before.astype(BF),
            (((0,), (0,)), ((), ())),
            preferred_element_type=F32,
        )
        lead = jnp.exp(turned_ref[...])
        for p in range(wide // LANES):
            lanes = slice(p * LANES, (p + 1) * LANES)
            first = (i * (wide // LANES) + p) * per
            leads = lane_halves([column(lead, first + j) for j in range(per)], LANES)
            ssd = inner_ref[:, lanes] + carried[:, lanes] * leads
            out_ref[:, lanes] = (ssd * jax.nn.silu(gate_ref[:, lanes].astype(F32))).astype(BF)

    whole = lambda a: pl.BlockSpec(a.shape, lambda i, s: (0, 0))
    block = pl.BlockSpec((rows, wide), lambda i, s: (0, i))
    thin = pl.BlockSpec((states + 8, wide), lambda i, s: (0, i))
    return pl.pallas_call(
        kernel,
        out_shape=jax.ShapeDtypeStruct((rows, channels), BF),
        grid_spec=pltpu.PrefetchScalarGridSpec(
            num_scalar_prefetch=1,
            grid=(channels // wide,),
            in_specs=[block, block, whole(output_map), whole(turned)] + [thin] * len(parts),
            out_specs=block,
        ),
        name="with_carried",
    )(seq.reshape(1), inner, mixer_gate, output_map, turned, *parts)


def mamba(grid, seq, mixer_input, mixer_gate, input_map, output_map, log_decay, skip_gain):
    cum, turned, own = local_states(mixer_input, input_map, log_decay)
    parts = [own]
    for k in range(1, grid.ns):
        parts.append(
            grid.swap(
                own,
                lambda x, c, z, y, k=k: ((x * 2 + c ^ k) // 2, (x * 2 + c ^ k) % 2, z, y),
            )
        )
    inner = inner_part(mixer_input, input_map, output_map, cum, turned, skip_gain)
    return with_carried(seq, inner, mixer_gate, output_map, turned, parts)


def activity(seq, pieces, gate_weight, up_weight, experts):
    part, packed = pieces[0].shape
    _, width, hidden = gate_weight.shape
    rows = part * len(pieces)
    wide = math.gcd(hidden, 256)

    def kernel(seq_ref, *refs):
        part_refs = refs[: len(pieces)]
        gate_ref, up_ref, out_ref, x_ref, tag_ref, sems = refs[len(pieces) :]

        @pl.when(pl.program_id(0) == 0)
        def _():
            copies = [
                pltpu.make_async_copy(ref, x_ref.at[pl.ds(i * part, part)], sems.at[i])
                for i, ref in enumerate(part_refs)
            ]
            for copy in copies:
                copy.start()
            for copy in copies:
                copy.wait()
            tags = x_ref[:, width:].astype(F32)
            lane = lax.broadcasted_iota(jnp.int32, tags.shape, 1)
            mine = (lane == seq_ref[0]) | (lane == seq_ref[0] + experts)
            tag = jnp.sum(jnp.where(mine, tags, 0.0), axis=1, keepdims=True)
            tag_ref[...] = jnp.broadcast_to(tag, tag_ref.shape)

        x = x_ref[:, :width]
        gate = jnp.dot(x, gate_ref[...], preferred_element_type=F32)
        up = jnp.dot(x, up_ref[...], preferred_element_type=F32)
        tag = jnp.concatenate([tag_ref[...]] * (wide // LANES), axis=1)
        out_ref[...] = (jax.nn.silu(gate) * up * tag).astype(BF)

    weight = pl.BlockSpec((None, width, wide), lambda i, s: (0, 0, i))
    return pl.pallas_call(
        kernel,
        out_shape=jax.ShapeDtypeStruct((rows, hidden), BF),
        grid_spec=pltpu.PrefetchScalarGridSpec(
            num_scalar_prefetch=1,
            grid=(hidden // wide,),
            in_specs=[pl.BlockSpec(memory_space=pl.ANY)] * len(pieces) + [weight, weight],
            out_specs=pl.BlockSpec((rows, wide), lambda i, s: (0, i)),
            scratch_shapes=[
                pltpu.VMEM((rows, packed), BF),
                pltpu.VMEM((rows, LANES), F32),
                pltpu.SemaphoreType.DMA((len(pieces),)),
            ],
        ),
        name="activity",
    )(seq.reshape(1), *pieces, gate_weight, up_weight)


def normalize(seq, h, t, parts, residual, norm_gain, router_weight, ids):
    width = residual.shape[1]
    half = parts[0].shape[1] // 2
    experts = router_weight.shape[0]

    def kernel(seq_ref, *refs):
        part_refs = refs[: len(parts)]
        residual_ref, gain_ref, router_ref, ids_ref, stream_ref, packed_ref = refs[len(parts) :]
        x_at, core = seq_ref[0] >> 1, seq_ref[0] & 1
        square = jnp.zeros((t, 1), F32)
        for x in range(len(parts)):
            for c in range(2):
                value = jnp.zeros((t, half), F32)
                for k, ref in enumerate(part_refs):
                    for j in range(2):
                        here = ((x_at ^ x) == k) & ((core ^ c) == j)
                        part = ref[:, j * half : (j + 1) * half].astype(F32)
                        value = jnp.where(here, part, value)
                lanes = slice((2 * x + c) * half, (2 * x + c + 1) * half)
                value = value + residual_ref[:, lanes].astype(F32)
                stream_ref[:, lanes] = value
                square = square + jnp.sum(value * value, axis=1, keepdims=True)
        scale = lax.rsqrt(square / width + epsilon)
        logits = [jnp.zeros((t, 1), F32)] * experts
        for i in range(2 * len(parts)):
            lanes = slice(i * half, (i + 1) * half)
            normed = (stream_ref[:, lanes] * scale * gain_ref[lanes][None, :]).astype(BF)
            packed_ref[:, lanes] = normed
            normed = normed.astype(F32)
            for e in range(experts):
                product = normed * router_ref[e : e + 1, lanes]
                logits[e] = logits[e] + jnp.sum(product, axis=1, keepdims=True)
        first, second = ids_ref[:, :1], ids_ref[:, 1:]
        left, right = jnp.zeros((t, 1), F32), jnp.zeros((t, 1), F32)
        for e in range(experts):
            left = jnp.where(first == e, logits[e], left)
            right = jnp.where(second == e, logits[e], right)
        lane = lax.broadcasted_iota(jnp.int32, (t, LANES), 1)
        expert = jnp.where(lane < experts, lane, lane - experts)
        gates = jnp.where(expert == first, jax.nn.sigmoid(left - right), 0.0) + jnp.where(
            expert == second, jax.nn.sigmoid(right - left), 0.0
        )
        high = gates.astype(BF)
        low = (gates - high.astype(F32)).astype(BF)
        packed_ref[:, width:] = jnp.where(lane < experts, high.astype(F32), low.astype(F32)).astype(BF)

    part = pl.BlockSpec((t, 2 * half), lambda i, s: (0, 0))
    return pl.pallas_call(
        kernel,
        out_shape=(
            jax.ShapeDtypeStruct((t, width), F32),
            jax.ShapeDtypeStruct((t, width + LANES), BF),
        ),
        grid_spec=pltpu.PrefetchScalarGridSpec(
            num_scalar_prefetch=1,
            grid=(1,),
            in_specs=[part] * len(parts)
            + [
                pl.BlockSpec((t, width), lambda i, s: (h, 0)),
                pl.BlockSpec((width,), lambda i, s: (0,)),
                pl.BlockSpec((experts, width), lambda i, s: (0, 0)),
                pl.BlockSpec((t, 2), lambda i, s: (h, 0)),
            ],
            out_specs=(
                pl.BlockSpec((t, width), lambda i, s: (0, 0)),
                pl.BlockSpec((t, width + LANES), lambda i, s: (0, 0)),
            ),
        ),
        name="normalize",
    )(seq.reshape(1), *parts, residual, norm_gain, router_weight, ids)


def shards(grid):
    n, nz = grid.n, grid.nz

    def run(
        mixer_input,
        mixer_gate,
        input_map,
        output_map,
        log_decay,
        skip_gain,
        out_proj,
        residual,
        norm_gain,
        router_weight,
        expert_ids,
        gate_weight,
        up_weight,
        down_weight,
    ):
        seq, exp = lax.axis_index("seq"), lax.axis_index("exp")
        y_at, z_at = exp % n, exp // n
        tok, width = residual.shape
        cols = out_proj.shape[1]
        chunks = CHUNKS if tok % (16 * CHUNKS) == 0 else 1
        t = tok // chunks
        other_proj = grid.over_core(out_proj)
        mixed = mamba(
            grid, seq, mixer_input, mixer_gate, input_map, output_map, log_decay, skip_gain
        )
        mixed = mixed.reshape(nz, n, chunks, t, -1)
        own_ids = lax.dynamic_slice_in_dim(expert_ids, exp * tok, tok, 0)
        experts = grid.ns

        def first_half(h, before):
            mine = jnp.stack(
                [
                    lax.dynamic_index_in_dim(mixed[:, :, h], y_at ^ k, 1, keepdims=False)
                    for k in range(n)
                ]
            ).reshape(n * nz * t, -1)
            parts = [mine] + [grid.over_x(mine, k) for k in range(1, n)]
            sums = []
            for part in parts:
                both = [
                    jnp.dot(part, weight, preferred_element_type=F32)
                    for weight in (out_proj, other_proj)
                ]
                sums.append(jnp.concatenate(both, axis=1).reshape(n, nz, t, 2 * cols))
            total = jnp.stack([s[0] for s in sums])
            for k in range(1, n):
                sent = jnp.stack([s[k] for s in sums]).astype(BF)
                got = grid.over_y(sent, k)
                total = total + got.astype(F32)
            at_z = [
                lax.dynamic_index_in_dim(total, z_at ^ k, 1, keepdims=False) for k in range(nz)
            ]
            got = [grid.over_z(at_z[k].astype(BF), k) for k in range(1, nz)]
            got, _ = lax.optimization_barrier((got, before))
            total = at_z[0] + sum(g.astype(F32) for g in got)
            parts = [total[0]] + [grid.over_x(total[k].astype(BF), k) for k in range(1, n)]
            stream, packed = normalize(
                seq, h, t, parts, residual, norm_gain, router_weight, own_ids
            )
            return stream, packed

        def spread(packed):
            held = [packed] + [grid.over_z(packed, k) for k in range(1, nz)]
            held = lax.optimization_barrier(jnp.concatenate(held, axis=0))
            got = [grid.over_xy(held, k) for k in range(1, n)]
            held = jnp.concatenate([held] + got, axis=0)
            mine = [held] + [grid.over_yx(held, k) for k in range(1, n)]
            pieces = []
            for piece in mine:
                pieces.append((piece, grid.over_core(piece)))
            return pieces

        def expert(pieces, joint):
            rows = pieces[0][0].shape[0]
            if joint:
                every = [p for piece in pieces for p in piece]
                every = activity(seq, every, gate_weight, up_weight, experts)
            outs = []
            for k in reversed(range(n)) if joint else range(n):
                if joint:
                    hidden = every[2 * k * rows : 2 * (k + 1) * rows]
                else:
                    hidden = activity(seq, pieces[k], gate_weight, up_weight, experts)
                out = jnp.dot(hidden, down_weight[0], preferred_element_type=F32)
                out = lax.optimization_barrier(out)
                outs.append((out[:rows], out[rows:].astype(BF)))
            return outs[::-1] if joint else outs

        def gather_back(outs):
            total = None
            for k, out in reversed(list(enumerate(outs))):
                got = grid.over_core(out[1])
                piece = out[0] + got.astype(F32)
                if k:
                    piece = grid.over_yx(piece.astype(BF), k).astype(F32)
                total = piece if total is None else total + piece
            total = total.reshape(n, -1, width)
            sent = total.astype(BF)
            total = total[0]
            for k in range(1, n):
                got = grid.over_xy(sent[k], k)
                total = total + got.astype(F32)
            total = total.reshape(nz, -1, width)
            got = [grid.over_z(total[k].astype(BF), k) for k in range(1, nz)]
            return total[0] + sum(g.astype(F32) for g in got)

        outs = []
        packed = residual
        for h in range(chunks):
            stream, packed = first_half(h, packed)
            done = expert(spread(packed), h > 0)
            outs.append((stream, gather_back(done)))
        outs = lax.optimization_barrier(outs)
        return jnp.concatenate([(stream + moe).astype(BF) for stream, moe in outs], axis=0)

    return run


def solution(mesh):
    return jax.shard_map(
        shards(Grid(mesh)),
        mesh=mesh,
        in_specs=(
            P("seq", "exp"),
            P("seq", "exp"),
            P(None, "seq"),
            P(None, "seq"),
            P("exp", "seq"),
            P("exp"),
            P("exp", "seq"),
            P(("seq", "exp"), None),
            P(),
            P(),
            P("seq", None),
            P("seq", None, "exp"),
            P("seq", None, "exp"),
            P("seq", "exp", None),
        ),
        out_specs=P(("seq", "exp"), None),
        check_vma=False,
    )
```
